32 devices in a mesh: seq: 16 (over z, x, core), chan: 2 (over y).
Axes of the slice: x: 2, y: 2, z: 4, core: 2. Of those that a mesh axis runs over, the one named last changes fastest.
Arguments:
- inputs: bfloat16 [4096, 2048], P('chan', 'seq'), may hold values from -6 to 6
- gating: bfloat16 [4096, 2048], P('chan', 'seq'), may hold values from -6 to 6
- grad_out: bfloat16 [4096, 2048], P('chan', 'seq'), may hold values from -6 to 6
- filters: float32 [64, 2048], P(None, ('seq', 'chan')), as said below
Outputs:
- grad_inputs: bfloat16 [4096, 2048], P('chan', 'seq')
- grad_gating: bfloat16 [4096, 2048], P('chan', 'seq')
- grad_filters: float32 [64, 2048], P(None, ('seq', 'chan'))
The draws below stay inside these ranges and needn't reach their ends.
Inputs may be any that keep to these rules, and one draw needn't show every extreme that they name: `filters`: every entry's magnitude is at most 0.77 times the square root of 131072.
All inputs are finite; a program needn't handle non-finite values.
Results may differ from the reference program's by a relative error of at most 0.0049.
Values may be sent and summed in bfloat16 or wider, within the bound.
A program may use at most 64 MiB of HBM per device.

```python
import math
import jax
import jax.numpy as jnp
from jax import lax

D = 4096
G = 64
GROUP_WIDTH = 64
LENGTH_OF_TEXT = 2048


def draw_filters(key, part):
    keys = jax.random.split(key, 6)
    ordinal_locations = jnp.arange(LENGTH_OF_TEXT, dtype=jnp.float32)[None, :]
    slow_share = 0.5
    retained_mask = jax.random.bernoulli(keys[0], slow_share, (G, 1))
    gradual_decay = jnp.exp(jax.random.uniform(keys[1], (G, 1), minval=math.log(0.05), maxval=0.0)) / LENGTH_OF_TEXT
    quick_decay = jnp.exp(jax.random.uniform(keys[2], (G, 1), minval=math.log(1.0 / 50.0), maxval=math.log(1.0 / 30.0)))
    pulse_count_per_unit = jnp.where(retained_mask, gradual_decay, quick_decay)
    spots = jax.random.randint(keys[3], (G, 2), 0, LENGTH_OF_TEXT).astype(jnp.float32)
    masking_draws = jax.random.uniform(keys[4], (G, 2), minval=0.5, maxval=0.8)
    forwarded_signal = ordinal_locations[:, :, None] >= spots[:, None, :]
    pulse_groupings = jnp.prod(jnp.where(forwarded_signal, masking_draws[:, None, :], 1.0), axis=-1)
    power_level = (1.0 - jnp.exp(-2.0 * pulse_count_per_unit)) / (1.0 - jnp.exp(-2.0 * pulse_count_per_unit * LENGTH_OF_TEXT))
    sinusoid_peak = jnp.sqrt(power_level * (GROUP_WIDTH * LENGTH_OF_TEXT))
    jitter_offset = jnp.clip(jax.random.normal(keys[5], (G, LENGTH_OF_TEXT)), -3.0, 3.0)
    return (jitter_offset * sinusoid_peak * jnp.exp(-pulse_count_per_unit * ordinal_locations) * pulse_groupings).astype(jnp.float32)


def steps_of(stream_key, extent, shards, least, top_value):
    def one(axis_at, shards_of):
        draws = jax.random.uniform(jax.random.fold_in(jax.random.fold_in(stream_key, 6), axis_at), (shards_of,), jnp.float32, least / len(shards), top_value / len(shards))
        return jnp.repeat(jnp.exp(draws), extent[axis_at] // shards_of).reshape((-1,) + (1,) * (len(extent) - axis_at - 1))

    level = one(*shards[0])
    for cut in shards[1:]:
        level = level * one(*cut)
    return level


def scatter_about(own_key, shape, width, reach, pieces=(), held_as=jnp.bfloat16):
    array = width * jax.random.normal(own_key, shape, jnp.float32)
    if pieces:
        array = array * steps_of(own_key, shape, pieces, -0.22, 0.18)
    return jnp.clip(array, -reach, reach).astype(held_as)


def setup_inputs(seed: int = 0) -> dict:
    streams_of = jax.random.split(jax.random.key(seed), 5)
    inputs = scatter_about(streams_of[0], (D, LENGTH_OF_TEXT), 1.0, 6.0, ((0, 2), (1, 16)))
    gating = scatter_about(streams_of[1], (D, LENGTH_OF_TEXT), 1.0, 6.0, ((0, 2), (1, 16)))
    grad_out = scatter_about(streams_of[2], (D, LENGTH_OF_TEXT), 1.0, 6.0, ((0, 2), (1, 16)))
    filters = draw_filters(jax.random.fold_in(streams_of[4], 71), 0)
    return dict(inputs=inputs, gating=gating, grad_out=grad_out, filters=filters)


def reference(inputs, gating, grad_out, filters):
    factor = 1.0 / math.sqrt(GROUP_WIDTH * LENGTH_OF_TEXT)
    padded = 2 * LENGTH_OF_TEXT

    def per_group(operands):
        values, gate_part, upstream, kernel = operands
        product_b = lax.optimization_barrier((gate_part.astype(jnp.float32) * upstream.astype(jnp.float32)).astype(jnp.bfloat16))
        product = product_b.astype(jnp.float32)
        spec_in = jnp.fft.rfft(values.astype(jnp.float32), n=padded, axis=-1)
        spec_up = jnp.fft.rfft(product, n=padded, axis=-1)
        spec_ker = jnp.fft.rfft(kernel * factor, n=padded)
        convolved = jnp.fft.irfft(spec_in * spec_ker[None, :], n=padded, axis=-1)[:, :LENGTH_OF_TEXT]
        conv_b = lax.optimization_barrier(convolved.astype(jnp.bfloat16))
        grad_gate = (upstream.astype(jnp.float32) * conv_b.astype(jnp.float32)).astype(jnp.bfloat16)
        grad_input = jnp.fft.irfft(spec_up * jnp.conj(spec_ker)[None, :], n=padded, axis=-1)[:, :LENGTH_OF_TEXT]
        grad_kernel = factor * jnp.fft.irfft(lax.optimization_barrier(jnp.sum(jnp.conj(spec_in) * spec_up, axis=0)), n=padded)[:LENGTH_OF_TEXT]
        return (grad_input.astype(jnp.bfloat16), grad_gate, grad_kernel)
    shaped = (inputs.reshape(G, GROUP_WIDTH, LENGTH_OF_TEXT), gating.reshape(G, GROUP_WIDTH, LENGTH_OF_TEXT), grad_out.reshape(G, GROUP_WIDTH, LENGTH_OF_TEXT), filters)
    grad_input, grad_gate, grad_kernel = lax.map(per_group, shaped)
    return (grad_input.reshape(D, LENGTH_OF_TEXT), grad_gate.reshape(D, LENGTH_OF_TEXT), grad_kernel)
```

```python
import functools
import math

import jax
import jax.numpy as jnp
from jax import lax
from jax.experimental import pallas as pl
from jax.experimental.pallas import tpu as pltpu
from jax.sharding import PartitionSpec as P

D = 4096
G = 64


HIGHEST = lax.Precision.HIGHEST


def make_tables(seq_count, block_len):
    outer = 2 * seq_count
    total = outer * block_len
    outer_index = jnp.arange(outer, dtype=jnp.int32)
    block_index = jnp.arange(seq_count, dtype=jnp.int32)
    inner_index = jnp.arange(block_len, dtype=jnp.int32)
    block_angle = (outer_index[:, None] * block_index[None, :] % outer).astype(jnp.float32) * (
        2.0 * math.pi / outer
    )
    twist_angle = (outer_index[:, None] * inner_index[None, :] % total).astype(jnp.float32) * (
        2.0 * math.pi / total
    )
    inner_angle = (inner_index[:, None] * inner_index[None, :] % block_len).astype(jnp.float32) * (
        2.0 * math.pi / block_len
    )
    return (
        jnp.cos(block_angle),
        jnp.sin(block_angle),
        jnp.cos(twist_angle),
        jnp.sin(twist_angle),
        jnp.cos(inner_angle),
        jnp.sin(inner_angle),
    )


def right_product(values, table):
    return jnp.einsum("ckm,mj->ckj", values, table, precision=HIGHEST)


def forward_dft(signal, tables):
    block_cos, block_sin, twist_cos, twist_sin, inner_cos, inner_sin = tables
    real_first = jnp.einsum("kn,cnm->ckm", block_cos, signal, precision=HIGHEST)
    imag_first = -jnp.einsum("kn,cnm->ckm", block_sin, signal, precision=HIGHEST)
    real_twist = real_first * twist_cos + imag_first * twist_sin
    imag_twist = imag_first * twist_cos - real_first * twist_sin
    real_spec = right_product(real_twist, inner_cos) + right_product(imag_twist, inner_sin)
    imag_spec = right_product(imag_twist, inner_cos) - right_product(real_twist, inner_sin)
    return (real_spec, imag_spec)


def inverse_dft(real_spec, imag_spec, tables):
    block_cos, block_sin, twist_cos, twist_sin, inner_cos, inner_sin = tables
    real_first = right_product(real_spec, inner_cos) - right_product(imag_spec, inner_sin)
    imag_first = right_product(real_spec, inner_sin) + right_product(imag_spec, inner_cos)
    real_twist = real_first * twist_cos - imag_first * twist_sin
    imag_twist = real_first * twist_sin + imag_first * twist_cos
    total = real_spec.shape[1] * real_spec.shape[2]
    result = jnp.einsum("kn,ckm->cnm", block_cos, real_twist, precision=HIGHEST)
    result = result - jnp.einsum("kn,ckm->cnm", block_sin, imag_twist, precision=HIGHEST)
    return result / total


def shards(inputs, gating, grad_out, filters):
    seq_count = lax.axis_size("seq")
    chan_count = lax.axis_size("chan")
    chan_rows, block_len = inputs.shape
    local_chan = chan_rows // seq_count
    group_width = D // G
    groups_here = G // chan_count
    local_groups = max(1, local_chan // group_width)
    group_share = local_chan // local_groups
    copies = max(1, seq_count // groups_here)
    length = block_len * seq_count
    outer = 2 * seq_count
    factor = 1.0 / math.sqrt(group_width * length)
    tables = make_tables(seq_count, block_len)
    whole = lax.all_gather(filters, ("seq", "chan"), axis=1, tiled=True)
    first_group = (
        lax.axis_index("chan") * chan_rows + lax.axis_index("seq") * local_chan
    ) // group_width
    kernel_rows = lax.dynamic_slice_in_dim(whole, first_group, local_groups, 0)
    kernel_blocks = kernel_rows.reshape(local_groups, seq_count, block_len)
    kernel_real, kernel_imag = forward_dft(kernel_blocks * factor, tables)
    kernel_real = kernel_real[:, None]
    kernel_imag = kernel_imag[:, None]
    shaped_inputs = inputs.reshape(chan_rows, 1, block_len)
    values, gate_part, upstream = (
        lax.all_to_all(shaped_inputs, "seq", split_axis=0, concat_axis=1, tiled=True),
        lax.all_to_all(
            gating.reshape(chan_rows, 1, block_len), "seq", split_axis=0, concat_axis=1, tiled=True
        ),
        lax.all_to_all(
            grad_out.reshape(chan_rows, 1, block_len),
            "seq",
            split_axis=0,
            concat_axis=1,
            tiled=True,
        ),
    )
    input_real, input_imag = forward_dft(values.astype(jnp.float32), tables)
    upstream_f = upstream.astype(jnp.float32)
    product_b = lax.optimization_barrier(
        (gate_part.astype(jnp.float32) * upstream_f).astype(jnp.bfloat16)
    )
    up_real, up_imag = forward_dft(product_b.astype(jnp.float32), tables)
    grouped_shape = (local_groups, group_share, outer, block_len)
    input_real = input_real.reshape(grouped_shape)
    input_imag = input_imag.reshape(grouped_shape)
    up_real = up_real.reshape(grouped_shape)
    up_imag = up_imag.reshape(grouped_shape)
    flat_shape = (local_chan, outer, block_len)
    conv_real = input_real * kernel_real - input_imag * kernel_imag
    conv_imag = input_real * kernel_imag + input_imag * kernel_real
    convolved = inverse_dft(conv_real.reshape(flat_shape), conv_imag.reshape(flat_shape), tables)
    conv_b = convolved.astype(jnp.bfloat16)
    second = (upstream_f * lax.optimization_barrier(conv_b).astype(jnp.float32)).astype(
        jnp.bfloat16
    )
    back_real = up_real * kernel_real + up_imag * kernel_imag
    back_imag = up_imag * kernel_real - up_real * kernel_imag
    grad_input = inverse_dft(
        back_real.reshape(flat_shape), back_imag.reshape(flat_shape), tables
    ).astype(jnp.bfloat16)
    returned_input, returned_second = (
        lax.all_to_all(grad_input, "seq", split_axis=1, concat_axis=0, tiled=True),
        lax.all_to_all(second, "seq", split_axis=1, concat_axis=0, tiled=True),
    )
    returned_second = returned_second.reshape(chan_rows, block_len)
    cross_real = jnp.sum(input_real * up_real + input_imag * up_imag, axis=1)
    cross_imag = jnp.sum(input_real * up_imag - input_imag * up_real, axis=1)
    partial_grad = inverse_dft(cross_real, cross_imag, tables) * factor
    received = lax.all_to_all(partial_grad, "seq", split_axis=1, concat_axis=0, tiled=True)
    summed = received.reshape(groups_here, copies, block_len).sum(axis=1)
    grad_filters = lax.all_to_all(summed, "chan", split_axis=1, concat_axis=0, tiled=True)
    return (returned_input.reshape(chan_rows, block_len), returned_second, grad_filters)


GROUP_WIDTH = D // G
MESH = pl.DeviceIdType.MESH
TILE = 256


def exchange_kernel(
    seq_count,
    chan_count,
    x_ref,
    gate_ref,
    up_ref,
    filt_ref,
    gi_ref,
    gg_ref,
    gf_ref,
    u_loc,
    xs,
    us,
    ks,
    cv,
    gv,
    acc_c,
    acc_g,
    conv_in,
    fg_out,
    x_send,
    x_recv,
    u_send,
    u_recv,
    k_send,
    k_recv,
    c_send,
    c_recv,
    g_send,
    g_recv,
    f_send,
    f_recv,
):
    seq = lax.axis_index("seq")
    chan = lax.axis_index("chan")
    everyone = seq_count * chan_count
    me = seq * chan_count + chan
    local_groups = xs.shape[0]
    block = x_ref.shape[1]
    per_tile = TILE // block
    length = block * seq_count
    tiles = length // TILE
    width = GROUP_WIDTH
    rows = tiles * width
    local_chan = local_groups * width

    barrier = pltpu.get_barrier_semaphore()

    def greet(k, carry):
        other = lax.rem(me + k, everyone)
        pl.semaphore_signal(
            barrier,
            inc=1,
            device_id=(other // chan_count, lax.rem(other, chan_count)),
            device_id_type=MESH,
        )
        return carry

    lax.fori_loop(1, everyone, greet, 0)
    pl.semaphore_wait(barrier, everyone - 1)

    def place(ref, g, s):
        return ref.at[
            g,
            pl.ds(pl.multiple_of((s // per_tile) * width, width), width),
            pl.ds(pl.multiple_of(lax.rem(s, per_tile) * block, block), block),
        ]

    def strip(ref, s, g):
        return ref.at[pl.ds(pl.multiple_of(s * local_chan + g * width, width), width), :]

    def forward(ref, buf, send, recv, g, to, slot_from):
        return pltpu.make_async_remote_copy(
            src_ref=strip(ref, to, g),
            dst_ref=place(buf, g, slot_from),
            send_sem=send.at[g, to],
            recv_sem=recv.at[g, slot_from],
            device_id=(to, chan),
            device_id_type=MESH,
        )

    def own(ref, buf, recv, g):
        return pltpu.make_async_copy(strip(ref, seq, g), place(buf, g, seq), recv.at[g, seq])

    def backward(buf, ref, send, recv, g, to, slot_from):
        return pltpu.make_async_remote_copy(
            src_ref=place(buf, g, to),
            dst_ref=strip(ref, slot_from, g),
            send_sem=send.at[g, to],
            recv_sem=recv.at[g, slot_from],
            device_id=(to, chan),
            device_id_type=MESH,
        )

    def own_back(buf, ref, recv, g):
        return pltpu.make_async_copy(place(buf, g, seq), strip(ref, seq, g), recv.at[g, seq])

    def filt_copy(to, slot_from):
        to_seq, to_chan = to // chan_count, lax.rem(to, chan_count)
        return pltpu.make_async_remote_copy(
            src_ref=filt_ref.at[to_chan * seq_count + to_seq],
            dst_ref=ks.at[slot_from],
            send_sem=k_send.at[to],
            recv_sem=k_recv.at[slot_from],
            device_id=(to_seq, to_chan),
            device_id_type=MESH,
        )

    def grad_copy(to, slot_from):
        to_seq, to_chan = to // chan_count, lax.rem(to, chan_count)
        from_seq, from_chan = slot_from // chan_count, lax.rem(slot_from, chan_count)
        return pltpu.make_async_remote_copy(
            src_ref=fg_out.at[to_seq],
            dst_ref=gf_ref.at[from_chan * seq_count + from_seq],
            send_sem=f_send.at[to],
            recv_sem=f_recv.at[slot_from],
            device_id=(to_seq, to_chan),
            device_id_type=MESH,
        )

    def seq_loop(body):
        def step(k, carry):
            body(lax.rem(seq + k, seq_count))
            return carry

        lax.fori_loop(1, seq_count, step, 0)

    def all_loop(body):
        def step(k, carry):
            body(lax.rem(me + k, everyone))
            return carry

        lax.fori_loop(1, everyone, step, 0)

    all_loop(lambda p: filt_copy(p, me).start())
    own_filt = pltpu.make_async_copy(
        filt_ref.at[chan * seq_count + seq], ks.at[me], k_recv.at[me]
    )
    own_filt.start()
    seq_loop(lambda p: forward(x_ref, xs, x_send, x_recv, 0, p, seq).start())
    own(x_ref, xs, x_recv, 0).start()

    u_loc[...] = (
        gate_ref[...].astype(jnp.float32) * up_ref[...].astype(jnp.float32)
    ).astype(jnp.bfloat16)
    seq_loop(lambda p: forward(u_loc, us, u_send, u_recv, 0, p, seq).start())
    own(u_loc, us, u_recv, 0).start()
    for g in range(1, local_groups):
        seq_loop(lambda p, g=g: forward(x_ref, xs, x_send, x_recv, g, p, seq).start())
        own(x_ref, xs, x_recv, g).start()
        seq_loop(lambda p, g=g: forward(u_loc, us, u_send, u_recv, g, p, seq).start())
        own(u_loc, us, u_recv, g).start()

    for g in range(local_groups):
        us[g, rows:, :] = jnp.zeros((rows, TILE), jnp.bfloat16)
    row_id = lax.broadcasted_iota(jnp.int32, (TILE, TILE), 0)
    col_id = lax.broadcasted_iota(jnp.int32, (TILE, TILE), 1)
    upper = col_id >= row_id
    flip = jnp.where(row_id + col_id == TILE - 1, 1.0, 0.0).astype(jnp.bfloat16)
    lower_flipped = col_id + row_id >= TILE - 1
    factor = 1.0 / math.sqrt(width * length)
    nt = (((1,), (1,)), ((), ()))
    nn = (((1,), (0,)), ((), ()))

    def dot(a, b, dims):
        return lax.dot_general(a, b, dims, preferred_element_type=jnp.float32)

    all_loop(lambda p: filt_copy(me, p).wait_recv())
    own_filt.wait()

    def group_step(g, carry):
        seq_loop(lambda p: forward(x_ref, xs, x_send, x_recv, g, seq, p).wait_recv())
        own(x_ref, xs, x_recv, g).wait()
        seq_loop(lambda p: forward(u_loc, us, u_send, u_recv, g, seq, p).wait_recv())
        own(u_loc, us, u_recv, g).wait()
        rolled_before = jnp.zeros((TILE, TILE), jnp.float32)
        for lag in range(tiles):
            pieces = []
            for q in range(per_tile):
                s = lag * per_tile + q
                part = ks[s * chan_count, pl.ds(g, 1), :]
                for c in range(1, chan_count):
                    part = part + ks[s * chan_count + c, pl.ds(g, 1), :]
                pieces.append(part)
            row = jnp.concatenate(pieces, axis=1)
            rolled = pltpu.roll(
                jnp.broadcast_to(row, (TILE, TILE)), 0, 1, stride=1, stride_axis=0
            )
            table = jnp.where(upper, rolled, rolled_before)
            rolled_before = rolled
            high = table.astype(jnp.bfloat16)
            low = (table - high.astype(jnp.float32)).astype(jnp.bfloat16)
            n = (tiles - lag) * width
            xin = xs[g, :n, :]
            uin = us[g, lag * width : rows, :]
            conv_add = dot(xin, high, nn) + dot(xin, low, nn)
            grad_add = dot(uin, high, nt) + dot(uin, low, nt)
            if lag == 0:
                acc_c[...] = conv_add
                acc_g[...] = grad_add
            else:
                acc_c[lag * width :, :] += conv_add
                acc_g[:n, :] += grad_add
        cv[g] = acc_c[...].astype(jnp.bfloat16)
        gv[g] = acc_g[...].astype(jnp.bfloat16)
        seq_loop(lambda p: backward(cv, conv_in, c_send, c_recv, g, p, seq).start())
        own_back(cv, conv_in, c_recv, g).start()
        seq_loop(lambda p: backward(gv, gi_ref, g_send, g_recv, g, p, seq).start())
        own_back(gv, gi_ref, g_recv, g).start()
        turned = dot(flip, xs[g], nt).astype(jnp.bfloat16)
        gram = dot(turned, us[g, 0:rows, :], nn)
        for lag in range(tiles):
            if lag + 1 < tiles:
                following = dot(turned, us[g, (lag + 1) * width : (lag + 1) * width + rows, :], nn)
            else:
                following = jnp.zeros_like(gram)
            mixed = jnp.where(lower_flipped, gram, following)
            gram = following
            aligned = pltpu.roll(mixed, 1, 1, stride=1, stride_axis=0)
            total = jnp.sum(aligned, axis=0, keepdims=True) * factor
            for q in range(per_tile):
                fg_out[lag * per_tile + q, pl.ds(g, 1), :] = total[:, q * block : (q + 1) * block]
        return carry

    lax.fori_loop(0, local_groups, group_step, 0)
    all_loop(lambda p: grad_copy(p, me).start())
    own_grad = pltpu.make_async_copy(
        fg_out.at[seq], gf_ref.at[chan * seq_count + seq], f_recv.at[me]
    )
    own_grad.start()

    for g in range(local_groups):
        seq_loop(lambda p, g=g: backward(cv, conv_in, c_send, c_recv, g, seq, p).wait_recv())
        own_back(cv, conv_in, c_recv, g).wait()
    gg_ref[...] = (up_ref[...].astype(jnp.float32) * conv_in[...].astype(jnp.float32)).astype(
        jnp.bfloat16
    )
    for g in range(local_groups):
        seq_loop(lambda p, g=g: backward(gv, gi_ref, g_send, g_recv, g, seq, p).wait_recv())
        own_back(gv, gi_ref, g_recv, g).wait()
    all_loop(lambda p: grad_copy(me, p).wait_recv())
    own_grad.wait()
    for g in range(local_groups):
        seq_loop(lambda p, g=g: forward(x_ref, xs, x_send, x_recv, g, p, seq).wait_send())
        seq_loop(lambda p, g=g: forward(u_loc, us, u_send, u_recv, g, p, seq).wait_send())
        seq_loop(lambda p, g=g: backward(cv, conv_in, c_send, c_recv, g, p, seq).wait_send())
        seq_loop(lambda p, g=g: backward(gv, gi_ref, g_send, g_recv, g, p, seq).wait_send())
    all_loop(lambda p: filt_copy(p, me).wait_send())
    all_loop(lambda p: grad_copy(p, me).wait_send())


def fused_shards(inputs, gating, grad_out, filters):
    seq_count = lax.axis_size("seq")
    chan_count = lax.axis_size("chan")
    chan_rows, block = inputs.shape
    everyone = seq_count * chan_count
    local_groups = chan_rows // seq_count // GROUP_WIDTH
    length = block * seq_count
    share = filters.shape[1]
    factor = 1.0 / math.sqrt(GROUP_WIDTH * length)
    chan = lax.axis_index("chan")
    scaled = (filters * factor).reshape(everyone, local_groups, share)
    lanes = jnp.tile(scaled, (1, 1, chan_count))
    held = lax.broadcasted_iota(jnp.int32, lanes.shape, 2) // share == chan
    packed = jnp.where(held, lanes, 0.0)
    packed = jnp.pad(packed, ((0, 0), (0, 8 - local_groups), (0, 0)))
    rows = length // TILE * GROUP_WIDTH
    vmem = pl.BlockSpec(memory_space=pltpu.VMEM)
    pair = pltpu.SemaphoreType.DMA((local_groups, seq_count))
    many = pltpu.SemaphoreType.DMA((everyone,))
    grad_inputs, grad_gating, grads = pl.pallas_call(
        functools.partial(exchange_kernel, seq_count, chan_count),
        out_shape=(
            jax.ShapeDtypeStruct((chan_rows, block), jnp.bfloat16),
            jax.ShapeDtypeStruct((chan_rows, block), jnp.bfloat16),
            jax.ShapeDtypeStruct((everyone, 8, block), jnp.float32),
        ),
        in_specs=[vmem] * 4,
        out_specs=(vmem, vmem, vmem),
        scratch_shapes=[
            pltpu.VMEM((chan_rows, block), jnp.bfloat16),
            pltpu.VMEM((local_groups, rows, TILE), jnp.bfloat16),
            pltpu.VMEM((local_groups, 2 * rows, TILE), jnp.bfloat16),
            pltpu.VMEM((everyone, 8, block), jnp.float32),
            pltpu.VMEM((local_groups, rows, TILE), jnp.bfloat16),
            pltpu.VMEM((local_groups, rows, TILE), jnp.bfloat16),
            pltpu.VMEM((rows, TILE), jnp.float32),
            pltpu.VMEM((rows, TILE), jnp.float32),
            pltpu.VMEM((chan_rows, block), jnp.bfloat16),
            pltpu.VMEM((seq_count, 8, block), jnp.float32),
            pair,
            pair,
            pair,
            pair,
            many,
            many,
            pair,
            pair,
            pair,
            pair,
            many,
            many,
        ],
        compiler_params=pltpu.CompilerParams(
            collective_id=0, has_side_effects=True, vmem_limit_bytes=40 * 1024 * 1024
        ),
    )(inputs, gating, grad_out, packed)
    grads = grads[:, :local_groups, :].reshape(G, block)
    grad_filters = lax.dynamic_slice_in_dim(grads, chan * share, share, 1)
    return (grad_inputs, grad_gating, grad_filters)


def solution(mesh):
    placed = (P("chan", "seq"), P("chan", "seq"), P("chan", "seq"), P(None, ("seq", "chan")))
    local_chan = D // mesh.shape["chan"] // mesh.shape["seq"]
    body = fused_shards if local_chan % GROUP_WIDTH == 0 else shards
    return jax.shard_map(
        body,
        mesh=mesh,
        in_specs=placed,
        out_specs=(P("chan", "seq"), P("chan", "seq"), P(None, ("seq", "chan"))),
        check_vma=False,
    )
```

```python
import functools
import math

import jax
import jax.numpy as jnp
from jax import lax
from jax.experimental import pallas as pl
from jax.experimental.pallas import tpu as pltpu
from jax.sharding import PartitionSpec as P

D = 4096
G = 64


HIGHEST = lax.Precision.HIGHEST


def make_tables(seq_count, block_len):
    outer = 2 * seq_count
    total = outer * block_len
    outer_index = jnp.arange(outer, dtype=jnp.int32)
    block_index = jnp.arange(seq_count, dtype=jnp.int32)
    inner_index = jnp.arange(block_len, dtype=jnp.int32)
    block_angle = (outer_index[:, None] * block_index[None, :] % outer).astype(jnp.float32) * (
        2.0 * math.pi / outer
    )
    twist_angle = (outer_index[:, None] * inner_index[None, :] % total).astype(jnp.float32) * (
        2.0 * math.pi / total
    )
    inner_angle = (inner_index[:, None] * inner_index[None, :] % block_len).astype(jnp.float32) * (
        2.0 * math.pi / block_len
    )
    return (
        jnp.cos(block_angle),
        jnp.sin(block_angle),
        jnp.cos(twist_angle),
        jnp.sin(twist_angle),
        jnp.cos(inner_angle),
        jnp.sin(inner_angle),
    )


def right_product(values, table):
    return jnp.einsum("ckm,mj->ckj", values, table, precision=HIGHEST)


def forward_dft(signal, tables):
    block_cos, block_sin, twist_cos, twist_sin, inner_cos, inner_sin = tables
    real_first = jnp.einsum("kn,cnm->ckm", block_cos, signal, precision=HIGHEST)
    imag_first = -jnp.einsum("kn,cnm->ckm", block_sin, signal, precision=HIGHEST)
    real_twist = real_first * twist_cos + imag_first * twist_sin
    imag_twist = imag_first * twist_cos - real_first * twist_sin
    real_spec = right_product(real_twist, inner_cos) + right_product(imag_twist, inner_sin)
    imag_spec = right_product(imag_twist, inner_cos) - right_product(real_twist, inner_sin)
    return (real_spec, imag_spec)


def inverse_dft(real_spec, imag_spec, tables):
    block_cos, block_sin, twist_cos, twist_sin, inner_cos, inner_sin = tables
    real_first = right_product(real_spec, inner_cos) - right_product(imag_spec, inner_sin)
    imag_first = right_product(real_spec, inner_sin) + right_product(imag_spec, inner_cos)
    real_twist = real_first * twist_cos - imag_first * twist_sin
    imag_twist = real_first * twist_sin + imag_first * twist_cos
    total = real_spec.shape[1] * real_spec.shape[2]
    result = jnp.einsum("kn,ckm->cnm", block_cos, real_twist, precision=HIGHEST)
    result = result - jnp.einsum("kn,ckm->cnm", block_sin, imag_twist, precision=HIGHEST)
    return result / total


def shards(inputs, gating, grad_out, filters):
    seq_count = lax.axis_size("seq")
    chan_count = lax.axis_size("chan")
    chan_rows, block_len = inputs.shape
    local_chan = chan_rows // seq_count
    group_width = D // G
    groups_here = G // chan_count
    local_groups = max(1, local_chan // group_width)
    group_share = local_chan // local_groups
    copies = max(1, seq_count // groups_here)
    length = block_len * seq_count
    outer = 2 * seq_count
    factor = 1.0 / math.sqrt(group_width * length)
    tables = make_tables(seq_count, block_len)
    whole = lax.all_gather(filters, ("seq", "chan"), axis=1, tiled=True)
    first_group = (
        lax.axis_index("chan") * chan_rows + lax.axis_index("seq") * local_chan
    ) // group_width
    kernel_rows = lax.dynamic_slice_in_dim(whole, first_group, local_groups, 0)
    kernel_blocks = kernel_rows.reshape(local_groups, seq_count, block_len)
    kernel_real, kernel_imag = forward_dft(kernel_blocks * factor, tables)
    kernel_real = kernel_real[:, None]
    kernel_imag = kernel_imag[:, None]
    shaped_inputs = inputs.reshape(chan_rows, 1, block_len)
    values, gate_part, upstream = (
        lax.all_to_all(shaped_inputs, "seq", split_axis=0, concat_axis=1, tiled=True),
        lax.all_to_all(
            gating.reshape(chan_rows, 1, block_len), "seq", split_axis=0, concat_axis=1, tiled=True
        ),
        lax.all_to_all(
            grad_out.reshape(chan_rows, 1, block_len),
            "seq",
            split_axis=0,
            concat_axis=1,
            tiled=True,
        ),
    )
    input_real, input_imag = forward_dft(values.astype(jnp.float32), tables)
    upstream_f = upstream.astype(jnp.float32)
    product_b = lax.optimization_barrier(
        (gate_part.astype(jnp.float32) * upstream_f).astype(jnp.bfloat16)
    )
    up_real, up_imag = forward_dft(product_b.astype(jnp.float32), tables)
    grouped_shape = (local_groups, group_share, outer, block_len)
    input_real = input_real.reshape(grouped_shape)
    input_imag = input_imag.reshape(grouped_shape)
    up_real = up_real.reshape(grouped_shape)
    up_imag = up_imag.reshape(grouped_shape)
    flat_shape = (local_chan, outer, block_len)
    conv_real = input_real * kernel_real - input_imag * kernel_imag
    conv_imag = input_real * kernel_imag + input_imag * kernel_real
    convolved = inverse_dft(conv_real.reshape(flat_shape), conv_imag.reshape(flat_shape), tables)
    conv_b = convolved.astype(jnp.bfloat16)
    second = (upstream_f * lax.optimization_barrier(conv_b).astype(jnp.float32)).astype(
        jnp.bfloat16
    )
    back_real = up_real * kernel_real + up_imag * kernel_imag
    back_imag = up_imag * kernel_real - up_real * kernel_imag
    grad_input = inverse_dft(
        back_real.reshape(flat_shape), back_imag.reshape(flat_shape), tables
    ).astype(jnp.bfloat16)
    returned_input, returned_second = (
        lax.all_to_all(grad_input, "seq", split_axis=1, concat_axis=0, tiled=True),
        lax.all_to_all(second, "seq", split_axis=1, concat_axis=0, tiled=True),
    )
    returned_second = returned_second.reshape(chan_rows, block_len)
    cross_real = jnp.sum(input_real * up_real + input_imag * up_imag, axis=1)
    cross_imag = jnp.sum(input_real * up_imag - input_imag * up_real, axis=1)
    partial_grad = inverse_dft(cross_real, cross_imag, tables) * factor
    received = lax.all_to_all(partial_grad, "seq", split_axis=1, concat_axis=0, tiled=True)
    summed = received.reshape(groups_here, copies, block_len).sum(axis=1)
    grad_filters = lax.all_to_all(summed, "chan", split_axis=1, concat_axis=0, tiled=True)
    return (returned_input.reshape(chan_rows, block_len), returned_second, grad_filters)


GROUP_WIDTH = D // G
MESH = pl.DeviceIdType.MESH
TILE = 256
LAYERS = 4
DELAY_B, DELAY_C, DELAY_D = 1, 2, 4


def layered_kernel(
    seq_count,
    chan_count,
    x_ref,
    gate_ref,
    up_ref,
    filt_ref,
    gi_ref,
    gg_ref,
    gf_ref,
    u_loc,
    xs,
    us,
    ks,
    cv,
    gv,
    acc_c,
    acc_g,
    conv_in,
    fg_out,
    held,
    part_out,
    part_in,
    x_send,
    x_recv,
    u_send,
    u_recv,
    c_send,
    c_recv,
    g_send,
    g_recv,
    z_send,
    z_recv,
    p_send,
    p_recv,
    k_send,
    k_recv,
    f_send,
    f_recv,
):
    seq = lax.axis_index("seq")
    chan = lax.axis_index("chan")
    peers = seq_count // LAYERS
    layer = seq // peers
    spot = lax.rem(seq, peers)
    last = LAYERS - 1
    everyone = seq_count * chan_count
    me = seq * chan_count + chan
    groups = xs.shape[0]
    block = x_ref.shape[1]
    per_tile = TILE // block
    length = block * seq_count
    tiles = length // TILE
    width = GROUP_WIDTH
    rows = tiles * width
    layer_rows = rows // LAYERS
    local_chan = groups * width

    barrier = pltpu.get_barrier_semaphore()

    def all_loop(body):
        def step(k, carry):
            body(lax.rem(me + k, everyone))
            return carry

        lax.fori_loop(1, everyone, step, 0)

    def peer_loop(body):
        for k in range(1, peers):
            body(lax.rem(spot + k, peers))

    def group_loop(body):
        def step(g, carry):
            body(g)
            return carry

        lax.fori_loop(0, groups, step, 0)

    def greet(p):
        pl.semaphore_signal(
            barrier,
            inc=1,
            device_id=(p // chan_count, lax.rem(p, chan_count)),
            device_id_type=MESH,
        )

    all_loop(greet)
    pl.semaphore_wait(barrier, everyone - 1)

    def place(ref, g, s):
        return ref.at[
            g,
            pl.ds(pl.multiple_of((s // per_tile) * width, width), width),
            pl.ds(pl.multiple_of(lax.rem(s, per_tile) * block, block), block),
        ]

    def strip(ref, q, g):
        return ref.at[pl.ds(pl.multiple_of(q * local_chan + g * width, width), width), :]

    def remote(src, dst, send, recv, to_seq, to_chan=None):
        return pltpu.make_async_remote_copy(
            src_ref=src,
            dst_ref=dst,
            send_sem=send,
            recv_sem=recv,
            device_id=(to_seq, chan if to_chan is None else to_chan),
            device_id_type=MESH,
        )

    def forward(ref, buf, send, recv, g, to, slot):
        return remote(
            strip(ref, to, g),
            place(buf, g, layer * peers + slot),
            send.at[g, to],
            recv.at[g, slot],
            layer * peers + to,
        )

    def own(ref, buf, recv, g):
        return pltpu.make_async_copy(strip(ref, spot, g), place(buf, g, seq), recv.at[g, spot])

    def backward(buf, ref, send, recv, g, to, slot):
        return remote(
            place(buf, g, to),
            strip(ref, slot, g),
            send.at[g, to],
            recv.at[g, slot],
            layer * peers + to,
        )

    def own_back(buf, ref, recv, g):
        return pltpu.make_async_copy(place(buf, g, spot), strip(ref, spot, g), recv.at[g, spot])

    def give_back(buf, ref, send, recv, g):
        peer_loop(lambda p: backward(buf, ref, send, recv, g, p, spot).start())
        own_back(buf, ref, recv, g).start()

    def take_back(buf, ref, send, recv, g):
        peer_loop(lambda p: backward(buf, ref, send, recv, g, spot, p).wait_recv())
        own_back(buf, ref, recv, g).wait()

    def hop(buf, g, which, step):
        ref = buf.at[g, pl.ds(which * layer_rows, layer_rows), :]
        to = jnp.clip(layer + step, 0, last) * peers + spot
        return remote(ref, ref, z_send.at[g, which], z_recv.at[g, which], to)

    def hand(g, step):
        to = jnp.clip(layer + step, 0, last) * peers + spot
        return remote(part_out.at[g], part_in.at[g], p_send.at[g], p_recv.at[g], to)

    def filt_copy(to, slot):
        to_seq, to_chan = to // chan_count, lax.rem(to, chan_count)
        return remote(
            filt_ref.at[to_chan * peers + lax.rem(to_seq, peers)],
            ks.at[slot],
            k_send.at[to],
            k_recv.at[slot],
            to_seq,
            to_chan,
        )

    def grad_copy(to, slot):
        to_seq, to_chan = to // chan_count, lax.rem(to, chan_count)
        from_seq, from_chan = slot // chan_count, lax.rem(slot, chan_count)
        return remote(
            fg_out.at[to_seq],
            gf_ref.at[from_chan * seq_count + from_seq],
            f_send.at[to],
            f_recv.at[slot],
            to_seq,
            to_chan,
        )

    def scatter(ref, buf, send, recv, g):
        peer_loop(lambda p: forward(ref, buf, send, recv, g, p, spot).start())
        own(ref, buf, recv, g).start()

    u_loc[...] = (
        gate_ref[...].astype(jnp.float32) * up_ref[...].astype(jnp.float32)
    ).astype(jnp.bfloat16)

    def scatter_both(g):
        scatter(x_ref, xs, x_send, x_recv, g)
        scatter(u_loc, us, u_send, u_recv, g)

    scatter_both(0)
    all_loop(lambda p: filt_copy(p, me).start())
    own_filt = pltpu.make_async_copy(filt_ref.at[chan * peers + spot], ks.at[me], k_recv.at[me])
    own_filt.start()

    def scatter_rest(g):
        @pl.when(g > 0)
        def _():
            scatter_both(g)

    group_loop(scatter_rest)

    for which in range(LAYERS):
        span = slice(which * layer_rows, (which + 1) * layer_rows)
        empty = jnp.zeros((groups, layer_rows, TILE), jnp.bfloat16)
        has_x = (layer == which) | ((layer > which) & (layer < last))
        has_u = (layer == which) | ((layer < which) & (layer > 0))

        @pl.when(jnp.logical_not(has_x))
        def _():
            xs[:, span, :] = empty

        @pl.when(jnp.logical_not(has_u))
        def _():
            us[:, span, :] = empty

    us[:, rows:, :] = jnp.zeros((groups, rows, TILE), jnp.bfloat16)
    row_id = lax.broadcasted_iota(jnp.int32, (TILE, TILE), 0)
    col_id = lax.broadcasted_iota(jnp.int32, (TILE, TILE), 1)
    upper = col_id >= row_id
    flip = jnp.where(row_id + col_id == TILE - 1, 1.0, 0.0).astype(jnp.bfloat16)
    lower_flipped = col_id + row_id >= TILE - 1
    columns = lax.broadcasted_iota(jnp.int32, (TILE, rows), 1)
    first = jnp.where(layer == 2, 2 * layer_rows, 0)
    end = jnp.where(layer == 2, 3 * layer_rows, rows)
    counted = (columns >= first) & (columns < end)
    factor = 1.0 / math.sqrt(width * length)
    nt = (((1,), (1,)), ((), ()))
    nn = (((1,), (0,)), ((), ()))
    mine = pl.ds(pl.multiple_of(layer * layer_rows, layer_rows), layer_rows)

    def dot(a, b, dims):
        return lax.dot_general(a, b, dims, preferred_element_type=jnp.float32)

    all_loop(lambda p: filt_copy(me, p).wait_recv())
    own_filt.wait()

    def gather_layer(g):
        peer_loop(lambda p: forward(x_ref, xs, x_send, x_recv, g, spot, p).wait_recv())
        own(x_ref, xs, x_recv, g).wait()
        peer_loop(lambda p: forward(u_loc, us, u_send, u_recv, g, spot, p).wait_recv())
        own(u_loc, us, u_recv, g).wait()
        for which in (0, 1):

            @pl.when(layer == which)
            def _():
                hop(xs, g, which, 1).start()

        for which in (2, 3):

            @pl.when(layer == which)
            def _():
                hop(us, g, which, -1).start()

    def relay(g):
        @pl.when(layer == 1)
        def _():
            hop(xs, g, 0, 1).wait_recv()
            hop(xs, g, 0, 1).start()

        @pl.when(layer == 2)
        def _():
            hop(us, g, 3, -1).wait_recv()
            hop(us, g, 3, -1).start()

    def compute(g):
        @pl.when(layer == 1)
        def _():
            hop(us, g, 2, -1).wait_recv()
            hop(us, g, 3, -1).wait_recv()

        @pl.when(layer == 2)
        def _():
            hop(xs, g, 1, 1).wait_recv()
            hop(xs, g, 0, 1).wait_recv()

        rolled_before = jnp.zeros((TILE, TILE), jnp.float32)
        for lag in range(tiles):
            pieces = []
            for q in range(per_tile):
                s = lag * per_tile + q
                part = ks[s * chan_count, pl.ds(g, 1), :]
                for c in range(1, chan_count):
                    part = part + ks[s * chan_count + c, pl.ds(g, 1), :]
                pieces.append(part)
            row = jnp.concatenate(pieces, axis=1)
            rolled = pltpu.roll(
                jnp.broadcast_to(row, (TILE, TILE)), 0, 1, stride=1, stride_axis=0
            )
            table = jnp.where(upper, rolled, rolled_before)
            rolled_before = rolled
            high = table.astype(jnp.bfloat16)
            low = (table - high.astype(jnp.float32)).astype(jnp.bfloat16)
            n = (tiles - lag) * width
            xin = xs[g, :n, :]
            uin = us[g, lag * width : rows, :]
            conv_add = dot(xin, high, nn) + dot(xin, low, nn)
            grad_add = dot(uin, high, nt) + dot(uin, low, nt)
            if lag == 0:
                acc_c[...] = conv_add
                acc_g[...] = grad_add
            else:
                acc_c[lag * width :, :] += conv_add
                acc_g[:n, :] += grad_add

        @pl.when(layer == 2)
        def _():
            part_out[g] = acc_c[last * layer_rows :, :]
            hand(g, 1).start()

        @pl.when(layer == 1)
        def _():
            part_out[g] = acc_g[:layer_rows, :]
            hand(g, -1).start()

        @pl.when(layer < last)
        def _():
            cv[g] = acc_c[mine, :].astype(jnp.bfloat16)
            give_back(cv, conv_in, c_send, c_recv, g)

        @pl.when(layer == last)
        def _():
            held[g] = acc_c[mine, :]

        @pl.when(layer > 0)
        def _():
            gv[g] = acc_g[mine, :].astype(jnp.bfloat16)
            give_back(gv, gi_ref, g_send, g_recv, g)

        @pl.when(layer == 0)
        def _():
            held[g] = acc_g[mine, :]

        turned = jnp.where(counted, dot(flip, xs[g], nt), 0.0).astype(jnp.bfloat16)
        gram = dot(turned, us[g, 0:rows, :], nn)
        for lag in range(tiles):
            if lag + 1 < tiles:
                start = (lag + 1) * width
                following = dot(turned, us[g, start : start + rows, :], nn)
            else:
                following = jnp.zeros_like(gram)
            mixed = jnp.where(lower_flipped, gram, following)
            gram = following
            aligned = pltpu.roll(mixed, 1, 1, stride=1, stride_axis=0)
            total = jnp.sum(aligned, axis=0, keepdims=True) * factor
            for q in range(per_tile):
                fg_out[lag * per_tile + q, pl.ds(g, 1), :] = total[:, q * block : (q + 1) * block]

    def finish(g):
        @pl.when(layer == last)
        def _():
            hand(g, 1).wait_recv()
            cv[g] = (held[g] + part_in[g]).astype(jnp.bfloat16)
            give_back(cv, conv_in, c_send, c_recv, g)

        @pl.when(layer == 0)
        def _():
            hand(g, -1).wait_recv()
            gv[g] = (held[g] + part_in[g]).astype(jnp.bfloat16)
            give_back(gv, gi_ref, g_send, g_recv, g)

    def stage(step, delay, body):
        @pl.when((step >= delay) & (step < groups + delay))
        def _():
            body(step - delay)

    def pipeline(step, carry):
        stage(step, 0, gather_layer)
        stage(step, DELAY_B, relay)
        stage(step, DELAY_C, compute)
        stage(step, DELAY_D, finish)
        return carry

    lax.fori_loop(0, groups + DELAY_C, pipeline, 0)
    all_loop(lambda p: grad_copy(p, me).start())
    own_grad = pltpu.make_async_copy(
        fg_out.at[seq], gf_ref.at[chan * seq_count + seq], f_recv.at[me]
    )
    own_grad.start()
    for g in range(groups + DELAY_C - DELAY_D, groups):
        finish(g)

    group_loop(lambda g: take_back(cv, conv_in, c_send, c_recv, g))
    gg_ref[...] = (up_ref[...].astype(jnp.float32) * conv_in[...].astype(jnp.float32)).astype(
        jnp.bfloat16
    )
    group_loop(lambda g: take_back(gv, gi_ref, g_send, g_recv, g))
    all_loop(lambda p: grad_copy(me, p).wait_recv())
    own_grad.wait()

    def drain(g):
        peer_loop(lambda p: forward(x_ref, xs, x_send, x_recv, g, p, spot).wait_send())
        peer_loop(lambda p: forward(u_loc, us, u_send, u_recv, g, p, spot).wait_send())
        peer_loop(lambda p: backward(cv, conv_in, c_send, c_recv, g, p, spot).wait_send())
        peer_loop(lambda p: backward(gv, gi_ref, g_send, g_recv, g, p, spot).wait_send())

        @pl.when(layer == 0)
        def _():
            hop(xs, g, 0, 1).wait_send()

        @pl.when(layer == 1)
        def _():
            hop(xs, g, 0, 1).wait_send()
            hop(xs, g, 1, 1).wait_send()
            hand(g, -1).wait_send()

        @pl.when(layer == 2)
        def _():
            hop(us, g, 2, -1).wait_send()
            hop(us, g, 3, -1).wait_send()
            hand(g, 1).wait_send()

        @pl.when(layer == 3)
        def _():
            hop(us, g, 3, -1).wait_send()

    group_loop(drain)
    all_loop(lambda p: filt_copy(p, me).wait_send())
    all_loop(lambda p: grad_copy(p, me).wait_send())


def layered_shards(inputs, gating, grad_out, filters):
    seq_count = lax.axis_size("seq")
    chan_count = lax.axis_size("chan")
    chan_rows, block = inputs.shape
    everyone = seq_count * chan_count
    peers = seq_count // LAYERS
    groups = chan_rows // peers // GROUP_WIDTH
    length = block * seq_count
    share = filters.shape[1]
    factor = 1.0 / math.sqrt(GROUP_WIDTH * length)
    chan = lax.axis_index("chan")
    lanes = jnp.tile(filters * factor, (1, chan_count))
    kept = lax.broadcasted_iota(jnp.int32, lanes.shape, 1) // share == chan
    packed = jnp.where(kept, lanes, 0.0).reshape(chan_count * peers, groups, block)
    rows = length // TILE * GROUP_WIDTH
    layer_rows = rows // LAYERS
    vmem = pl.BlockSpec(memory_space=pltpu.VMEM)
    pair = pltpu.SemaphoreType.DMA((groups, peers))
    stacked = pltpu.SemaphoreType.DMA((groups, LAYERS))
    single = pltpu.SemaphoreType.DMA((groups,))
    many = pltpu.SemaphoreType.DMA((everyone,))
    grad_inputs, grad_gating, grads = pl.pallas_call(
        functools.partial(layered_kernel, seq_count, chan_count),
        out_shape=(
            jax.ShapeDtypeStruct((chan_rows, block), jnp.bfloat16),
            jax.ShapeDtypeStruct((chan_rows, block), jnp.bfloat16),
            jax.ShapeDtypeStruct((everyone, groups, block), jnp.float32),
        ),
        in_specs=[vmem] * 4,
        out_specs=(vmem, vmem, vmem),
        scratch_shapes=[
            pltpu.VMEM((chan_rows, block), jnp.bfloat16),
            pltpu.VMEM((groups, rows, TILE), jnp.bfloat16),
            pltpu.VMEM((groups, 2 * rows, TILE), jnp.bfloat16),
            pltpu.VMEM((everyone, groups, block), jnp.float32),
            pltpu.VMEM((groups, layer_rows, TILE), jnp.bfloat16),
            pltpu.VMEM((groups, layer_rows, TILE), jnp.bfloat16),
            pltpu.VMEM((rows, TILE), jnp.float32),
            pltpu.VMEM((rows, TILE), jnp.float32),
            pltpu.VMEM((chan_rows, block), jnp.bfloat16),
            pltpu.VMEM((seq_count, groups, block), jnp.float32),
            pltpu.VMEM((groups, layer_rows, TILE), jnp.float32),
            pltpu.VMEM((groups, layer_rows, TILE), jnp.float32),
            pltpu.VMEM((groups, layer_rows, TILE), jnp.float32),
        ]
        + [pair] * 8
        + [stacked] * 2
        + [single] * 2
        + [many] * 4,
        compiler_params=pltpu.CompilerParams(
            collective_id=0, has_side_effects=True, vmem_limit_bytes=40 * 1024 * 1024
        ),
    )(inputs, gating, grad_out, packed)
    grads = grads.reshape(chan_count, LAYERS, peers * groups, block).sum(axis=1)
    grads = grads.reshape(G, block)
    grad_filters = lax.dynamic_slice_in_dim(grads, chan * share, share, 1)
    return (grad_inputs, grad_gating, grad_filters)


def solution(mesh):
    placed = (P("chan", "seq"), P("chan", "seq"), P("chan", "seq"), P(None, ("seq", "chan")))
    layered = mesh.shape["seq"] == 16 and mesh.shape["chan"] == 2
    return jax.shard_map(
        layered_shards if layered else shards,
        mesh=mesh,
        in_specs=placed,
        out_specs=(P("chan", "seq"), P("chan", "seq"), P(None, ("seq", "chan"))),
        check_vma=False,
    )
```

```python
import functools
import math

import jax
import jax.numpy as jnp
from jax import lax
from jax.experimental import pallas as pl
from jax.experimental.pallas import tpu as pltpu
from jax.sharding import PartitionSpec as P

D = 4096
G = 64


HIGHEST = lax.Precision.HIGHEST


def make_tables(seq_count, block_len):
    outer = 2 * seq_count
    total = outer * block_len
    outer_index = jnp.arange(outer, dtype=jnp.int32)
    block_index = jnp.arange(seq_count, dtype=jnp.int32)
    inner_index = jnp.arange(block_len, dtype=jnp.int32)
    block_angle = (outer_index[:, None] * block_index[None, :] % outer).astype(jnp.float32) * (
        2.0 * math.pi / outer
    )
    twist_angle = (outer_index[:, None] * inner_index[None, :] % total).astype(jnp.float32) * (
        2.0 * math.pi / total
    )
    inner_angle = (inner_index[:, None] * inner_index[None, :] % block_len).astype(jnp.float32) * (
        2.0 * math.pi / block_len
    )
    return (
        jnp.cos(block_angle),
        jnp.sin(block_angle),
        jnp.cos(twist_angle),
        jnp.sin(twist_angle),
        jnp.cos(inner_angle),
        jnp.sin(inner_angle),
    )


def right_product(values, table):
    return jnp.einsum("ckm,mj->ckj", values, table, precision=HIGHEST)


def forward_dft(signal, tables):
    block_cos, block_sin, twist_cos, twist_sin, inner_cos, inner_sin = tables
    real_first = jnp.einsum("kn,cnm->ckm", block_cos, signal, precision=HIGHEST)
    imag_first = -jnp.einsum("kn,cnm->ckm", block_sin, signal, precision=HIGHEST)
    real_twist = real_first * twist_cos + imag_first * twist_sin
    imag_twist = imag_first * twist_cos - real_first * twist_sin
    real_spec = right_product(real_twist, inner_cos) + right_product(imag_twist, inner_sin)
    imag_spec = right_product(imag_twist, inner_cos) - right_product(real_twist, inner_sin)
    return (real_spec, imag_spec)


def inverse_dft(real_spec, imag_spec, tables):
    block_cos, block_sin, twist_cos, twist_sin, inner_cos, inner_sin = tables
    real_first = right_product(real_spec, inner_cos) - right_product(imag_spec, inner_sin)
    imag_first = right_product(real_spec, inner_sin) + right_product(imag_spec, inner_cos)
    real_twist = real_first * twist_cos - imag_first * twist_sin
    imag_twist = real_first * twist_sin + imag_first * twist_cos
    total = real_spec.shape[1] * real_spec.shape[2]
    result = jnp.einsum("kn,ckm->cnm", block_cos, real_twist, precision=HIGHEST)
    result = result - jnp.einsum("kn,ckm->cnm", block_sin, imag_twist, precision=HIGHEST)
    return result / total


def shards(inputs, gating, grad_out, filters):
    seq_count = lax.axis_size("seq")
    chan_count = lax.axis_size("chan")
    chan_rows, block_len = inputs.shape
    local_chan = chan_rows // seq_count
    group_width = D // G
    groups_here = G // chan_count
    local_groups = max(1, local_chan // group_width)
    group_share = local_chan // local_groups
    copies = max(1, seq_count // groups_here)
    length = block_len * seq_count
    outer = 2 * seq_count
    factor = 1.0 / math.sqrt(group_width * length)
    tables = make_tables(seq_count, block_len)
    whole = lax.all_gather(filters, ("seq", "chan"), axis=1, tiled=True)
    first_group = (
        lax.axis_index("chan") * chan_rows + lax.axis_index("seq") * local_chan
    ) // group_width
    kernel_rows = lax.dynamic_slice_in_dim(whole, first_group, local_groups, 0)
    kernel_blocks = kernel_rows.reshape(local_groups, seq_count, block_len)
    kernel_real, kernel_imag = forward_dft(kernel_blocks * factor, tables)
    kernel_real = kernel_real[:, None]
    kernel_imag = kernel_imag[:, None]
    shaped_inputs = inputs.reshape(chan_rows, 1, block_len)
    values, gate_part, upstream = (
        lax.all_to_all(shaped_inputs, "seq", split_axis=0, concat_axis=1, tiled=True),
        lax.all_to_all(
            gating.reshape(chan_rows, 1, block_len), "seq", split_axis=0, concat_axis=1, tiled=True
        ),
        lax.all_to_all(
            grad_out.reshape(chan_rows, 1, block_len),
            "seq",
            split_axis=0,
            concat_axis=1,
            tiled=True,
        ),
    )
    input_real, input_imag = forward_dft(values.astype(jnp.float32), tables)
    upstream_f = upstream.astype(jnp.float32)
    product_b = lax.optimization_barrier(
        (gate_part.astype(jnp.float32) * upstream_f).astype(jnp.bfloat16)
    )
    up_real, up_imag = forward_dft(product_b.astype(jnp.float32), tables)
    grouped_shape = (local_groups, group_share, outer, block_len)
    input_real = input_real.reshape(grouped_shape)
    input_imag = input_imag.reshape(grouped_shape)
    up_real = up_real.reshape(grouped_shape)
    up_imag = up_imag.reshape(grouped_shape)
    flat_shape = (local_chan, outer, block_len)
    conv_real = input_real * kernel_real - input_imag * kernel_imag
    conv_imag = input_real * kernel_imag + input_imag * kernel_real
    convolved = inverse_dft(conv_real.reshape(flat_shape), conv_imag.reshape(flat_shape), tables)
    conv_b = convolved.astype(jnp.bfloat16)
    second = (upstream_f * lax.optimization_barrier(conv_b).astype(jnp.float32)).astype(
        jnp.bfloat16
    )
    back_real = up_real * kernel_real + up_imag * kernel_imag
    back_imag = up_imag * kernel_real - up_real * kernel_imag
    grad_input = inverse_dft(
        back_real.reshape(flat_shape), back_imag.reshape(flat_shape), tables
    ).astype(jnp.bfloat16)
    returned_input, returned_second = (
        lax.all_to_all(grad_input, "seq", split_axis=1, concat_axis=0, tiled=True),
        lax.all_to_all(second, "seq", split_axis=1, concat_axis=0, tiled=True),
    )
    returned_second = returned_second.reshape(chan_rows, block_len)
    cross_real = jnp.sum(input_real * up_real + input_imag * up_imag, axis=1)
    cross_imag = jnp.sum(input_real * up_imag - input_imag * up_real, axis=1)
    partial_grad = inverse_dft(cross_real, cross_imag, tables) * factor
    received = lax.all_to_all(partial_grad, "seq", split_axis=1, concat_axis=0, tiled=True)
    summed = received.reshape(groups_here, copies, block_len).sum(axis=1)
    grad_filters = lax.all_to_all(summed, "chan", split_axis=1, concat_axis=0, tiled=True)
    return (returned_input.reshape(chan_rows, block_len), returned_second, grad_filters)


GROUP_WIDTH = D // G
MESH = pl.DeviceIdType.MESH
TILE = 256
LAYERS = 4
DELAY_B, DELAY_C, DELAY_D = 1, 2, 4


def layered_kernel(
    seq_count,
    chan_count,
    x_ref,
    gate_hbm,
    up_hbm,
    raw_ref,
    gi_ref,
    gg_ref,
    grad_ref,
    gate_ref,
    up_ref,
    filt_ref,
    gf_ref,
    u_loc,
    xs,
    us,
    ks,
    cv,
    gv,
    acc_c,
    acc_g,
    conv_in,
    fg_out,
    held,
    part_out,
    part_in,
    x_send,
    x_recv,
    u_send,
    u_recv,
    c_send,
    c_recv,
    g_send,
    g_recv,
    z_send,
    z_recv,
    p_send,
    p_recv,
    k_send,
    k_recv,
    f_send,
    f_recv,
    in_sem,
):
    seq = lax.axis_index("seq")
    chan = lax.axis_index("chan")
    peers = seq_count // LAYERS
    layer = seq // peers
    spot = lax.rem(seq, peers)
    last = LAYERS - 1
    everyone = seq_count * chan_count
    me = seq * chan_count + chan
    groups = xs.shape[0]
    block = x_ref.shape[1]
    per_tile = TILE // block
    length = block * seq_count
    tiles = length // TILE
    width = GROUP_WIDTH
    rows = tiles * width
    layer_rows = rows // LAYERS
    local_chan = groups * width

    barrier = pltpu.get_barrier_semaphore()

    def all_loop(body):
        def step(k, carry):
            body(lax.rem(me + k, everyone))
            return carry

        lax.fori_loop(1, everyone, step, 0)

    def peer_loop(body):
        for k in range(1, peers):
            body(lax.rem(spot + k, peers))

    def group_loop(body):
        def step(g, carry):
            body(g)
            return carry

        lax.fori_loop(0, groups, step, 0)

    def greet(p):
        pl.semaphore_signal(
            barrier,
            inc=1,
            device_id=(p // chan_count, lax.rem(p, chan_count)),
            device_id_type=MESH,
        )

    gate_in = pltpu.make_async_copy(gate_hbm, gate_ref, in_sem.at[0])
    up_in = pltpu.make_async_copy(up_hbm, up_ref, in_sem.at[1])
    gate_in.start()
    up_in.start()
    all_loop(greet)
    share = raw_ref.shape[1]
    factor = 1.0 / math.sqrt(width * length)
    scaled = raw_ref[...] * factor
    lanes = jnp.concatenate([scaled] * chan_count, axis=1)
    kept = lax.broadcasted_iota(jnp.int32, lanes.shape, 1) // share == chan
    lanes = jnp.where(kept, lanes, 0.0)
    for i in range(chan_count * peers):
        filt_ref[i] = lanes[i * groups : (i + 1) * groups, :]
    gate_in.wait()
    up_in.wait()
    u_loc[...] = (
        gate_ref[...].astype(jnp.float32) * up_ref[...].astype(jnp.float32)
    ).astype(jnp.bfloat16)
    fg_out[...] = jnp.zeros_like(fg_out)
    pl.semaphore_wait(barrier, everyone - 1)

    def place(ref, g, s):
        return ref.at[
            g,
            pl.ds(pl.multiple_of((s // per_tile) * width, width), width),
            pl.ds(pl.multiple_of(lax.rem(s, per_tile) * block, block), block),
        ]

    def strip(ref, q, g):
        return ref.at[pl.ds(pl.multiple_of(q * local_chan + g * width, width), width), :]

    def remote(src, dst, send, recv, to_seq, to_chan=None):
        return pltpu.make_async_remote_copy(
            src_ref=src,
            dst_ref=dst,
            send_sem=send,
            recv_sem=recv,
            device_id=(to_seq, chan if to_chan is None else to_chan),
            device_id_type=MESH,
        )

    def forward(ref, buf, send, recv, g, to, slot):
        return remote(
            strip(ref, to, g),
            place(buf, g, layer * peers + slot),
            send.at[g, to],
            recv.at[g, slot],
            layer * peers + to,
        )

    def own(ref, buf, recv, g):
        return pltpu.make_async_copy(strip(ref, spot, g), place(buf, g, seq), recv.at[g, spot])

    def backward(buf, ref, send, recv, g, to, slot):
        return remote(
            place(buf, g, to),
            strip(ref, slot, g),
            send.at[g, to],
            recv.at[g, slot],
            layer * peers + to,
        )

    def own_back(buf, ref, recv, g):
        return pltpu.make_async_copy(place(buf, g, spot), strip(ref, spot, g), recv.at[g, spot])

    def give_back(buf, ref, send, recv, g):
        peer_loop(lambda p: backward(buf, ref, send, recv, g, p, spot).start())
        own_back(buf, ref, recv, g).start()

    def take_back(buf, ref, send, recv, g):
        peer_loop(lambda p: backward(buf, ref, send, recv, g, spot, p).wait_recv())
        own_back(buf, ref, recv, g).wait()

    def hop(buf, g, which, step):
        ref = buf.at[g, pl.ds(which * layer_rows, layer_rows), :]
        to = jnp.clip(layer + step, 0, last) * peers + spot
        return remote(ref, ref, z_send.at[g, which], z_recv.at[g, which], to)

    def hand(g, step):
        to = jnp.clip(layer + step, 0, last) * peers + spot
        return remote(part_out.at[g], part_in.at[g], p_send.at[g], p_recv.at[g], to)

    def filt_copy(to, slot):
        to_seq, to_chan = to // chan_count, lax.rem(to, chan_count)
        return remote(
            filt_ref.at[to_chan * peers + lax.rem(to_seq, peers)],
            ks.at[slot],
            k_send.at[to],
            k_recv.at[slot],
            to_seq,
            to_chan,
        )

    def grad_copy(to, slot):
        to_seq, to_chan = to // chan_count, lax.rem(to, chan_count)
        from_seq, from_chan = slot // chan_count, lax.rem(slot, chan_count)
        return remote(
            fg_out.at[to_seq],
            gf_ref.at[from_chan * seq_count + from_seq],
            f_send.at[to],
            f_recv.at[slot],
            to_seq,
            to_chan,
        )

    def scatter(ref, buf, send, recv, g):
        peer_loop(lambda p: forward(ref, buf, send, recv, g, p, spot).start())
        own(ref, buf, recv, g).start()

    def scatter_both(g):
        scatter(x_ref, xs, x_send, x_recv, g)
        scatter(u_loc, us, u_send, u_recv, g)

    scatter_both(0)
    all_loop(lambda p: filt_copy(p, me).start())
    own_filt = pltpu.make_async_copy(filt_ref.at[chan * peers + spot], ks.at[me], k_recv.at[me])
    own_filt.start()

    def scatter_rest(g):
        @pl.when(g > 0)
        def _():
            scatter_both(g)

    group_loop(scatter_rest)

    for which in range(LAYERS):
        span = slice(which * layer_rows, (which + 1) * layer_rows)
        empty = jnp.zeros((groups, layer_rows, TILE), jnp.bfloat16)
        has_u = (layer == which) | ((layer < which) & (layer > 0))

        @pl.when(jnp.logical_not(has_u))
        def _():
            us[:, span, :] = empty

    us[:, rows:, :] = jnp.zeros((groups, rows, TILE), jnp.bfloat16)
    row_id = lax.broadcasted_iota(jnp.int32, (TILE, TILE), 0)
    col_id = lax.broadcasted_iota(jnp.int32, (TILE, TILE), 1)
    upper = col_id >= row_id
    flip = jnp.where(row_id + col_id == TILE - 1, 1.0, 0.0).astype(jnp.bfloat16)
    lower_flipped = col_id + row_id >= TILE - 1
    nt = (((1,), (1,)), ((), ()))
    nn = (((1,), (0,)), ((), ()))
    half = tiles // LAYERS

    def dot(a, b, dims):
        return lax.dot_general(a, b, dims, preferred_element_type=jnp.float32)

    def gather_layer(g):
        peer_loop(lambda p: forward(x_ref, xs, x_send, x_recv, g, spot, p).wait_recv())
        own(x_ref, xs, x_recv, g).wait()
        peer_loop(lambda p: forward(u_loc, us, u_send, u_recv, g, spot, p).wait_recv())
        own(u_loc, us, u_recv, g).wait()
        for which in (0, 1):

            @pl.when(layer == which)
            def _():
                hop(xs, g, which, 1).start()

        for which in (2, 3):

            @pl.when(layer == which)
            def _():
                hop(us, g, which, -1).start()

    def relay(g):
        @pl.when(layer == 1)
        def _():
            hop(xs, g, 0, 1).wait_recv()
            hop(xs, g, 0, 1).start()

        @pl.when(layer == 2)
        def _():
            hop(us, g, 3, -1).wait_recv()
            hop(us, g, 3, -1).start()

    def compute(g):
        @pl.when(g == 0)
        def _():
            all_loop(lambda p: filt_copy(me, p).wait_recv())
            own_filt.wait()

        for which in range(LAYERS):

            @pl.when(layer == which)
            def _(which=which):
                compute_for(which, g)

    def compute_for(which, g):
        low_end, high_end = which * half, (which + 1) * half - 1
        x_first = low_end if which == last else 0
        u_last = high_end if which == 0 else tiles - 1
        conv_last = tiles - 1 if which == 2 else high_end
        grad_first = 0 if which == 1 else low_end
        gram_first = 0 if which == 1 else low_end
        if which == 1:
            hop(us, g, 2, -1).wait_recv()
            hop(us, g, 3, -1).wait_recv()
        if which == 2:
            hop(xs, g, 1, 1).wait_recv()
            hop(xs, g, 0, 1).wait_recv()

        def span(first, final):
            return slice(first * width, (final + 1) * width)

        acc_c[span(low_end, conv_last), :] = jnp.zeros(
            ((conv_last - low_end + 1) * width, TILE), jnp.float32
        )
        acc_g[span(grad_first, high_end), :] = jnp.zeros(
            ((high_end - grad_first + 1) * width, TILE), jnp.float32
        )
        rolled_before = jnp.zeros((TILE, TILE), jnp.float32)
        for lag in range(tiles):
            first, final = max(x_first, low_end - lag), min(high_end, conv_last - lag)
            u_from, u_to = max(low_end, grad_first + lag), min(u_last, high_end + lag)
            if first > final and u_from > u_to:
                break
            pieces = []
            for q in range(per_tile):
                s = lag * per_tile + q
                part = ks[s * chan_count, pl.ds(g, 1), :]
                for c in range(1, chan_count):
                    part = part + ks[s * chan_count + c, pl.ds(g, 1), :]
                pieces.append(part)
            row = jnp.concatenate(pieces, axis=1)
            rolled = pltpu.roll(
                jnp.broadcast_to(row, (TILE, TILE)), 0, 1, stride=1, stride_axis=0
            )
            table = jnp.where(upper, rolled, rolled_before)
            rolled_before = rolled
            high = table.astype(jnp.bfloat16)
            low = (table - high.astype(jnp.float32)).astype(jnp.bfloat16)
            if first <= final:
                xin = xs[g, span(first, final), :]
                acc_c[span(first + lag, final + lag), :] += dot(xin, high, nn) + dot(xin, low, nn)
            if u_from <= u_to:
                uin = us[g, span(u_from, u_to), :]
                acc_g[span(u_from - lag, u_to - lag), :] += dot(uin, high, nt) + dot(uin, low, nt)

        mine = span(low_end, high_end)
        if which == 2:
            part_out[g] = acc_c[last * layer_rows :, :]
            hand(g, 1).start()
        if which == 1:
            part_out[g] = acc_g[:layer_rows, :]
            hand(g, -1).start()
        if which < last:
            cv[g] = acc_c[mine, :].astype(jnp.bfloat16)
            give_back(cv, conv_in, c_send, c_recv, g)
        else:
            held[g] = acc_c[mine, :]
        if which > 0:
            gv[g] = acc_g[mine, :].astype(jnp.bfloat16)
            give_back(gv, gi_ref, g_send, g_recv, g)
        else:
            held[g] = acc_g[mine, :]

        x_span = span(gram_first, high_end)
        x_rows = (high_end - gram_first + 1) * width
        turned = dot(flip, xs[g, x_span, :], nt).astype(jnp.bfloat16)

        def gram_of(lag):
            start = (gram_first + lag) * width
            return dot(turned, us[g, start : start + x_rows, :], nn)

        gram = gram_of(0)
        final_lag = u_last - gram_first
        for lag in range(final_lag + 1):
            following = gram_of(lag + 1) if lag < final_lag else jnp.zeros_like(gram)
            mixed = jnp.where(lower_flipped, gram, following)
            gram = following
            aligned = pltpu.roll(mixed, 1, 1, stride=1, stride_axis=0)
            total = jnp.sum(aligned, axis=0, keepdims=True) * factor
            for q in range(per_tile):
                fg_out[lag * per_tile + q, pl.ds(g, 1), :] = total[:, q * block : (q + 1) * block]

    def finish(g):
        @pl.when(layer == last)
        def _():
            hand(g, 1).wait_recv()
            cv[g] = (held[g] + part_in[g]).astype(jnp.bfloat16)
            give_back(cv, conv_in, c_send, c_recv, g)

        @pl.when(layer == 0)
        def _():
            hand(g, -1).wait_recv()
            gv[g] = (held[g] + part_in[g]).astype(jnp.bfloat16)
            give_back(gv, gi_ref, g_send, g_recv, g)

    def stage(step, delay, body):
        @pl.when((step >= delay) & (step < groups + delay))
        def _():
            body(step - delay)

    def pipeline(step, carry):
        stage(step, 0, gather_layer)
        stage(step, DELAY_B, relay)
        stage(step, DELAY_C, compute)
        stage(step, DELAY_D, finish)
        return carry

    lax.fori_loop(0, groups + DELAY_C, pipeline, 0)
    all_loop(lambda p: grad_copy(p, me).start())
    own_grad = pltpu.make_async_copy(
        fg_out.at[seq], gf_ref.at[chan * seq_count + seq], f_recv.at[me]
    )
    own_grad.start()
    for g in range(groups + DELAY_C - DELAY_D, groups):
        finish(g)

    group_loop(lambda g: take_back(cv, conv_in, c_send, c_recv, g))
    gg_ref[...] = (up_ref[...].astype(jnp.float32) * conv_in[...].astype(jnp.float32)).astype(
        jnp.bfloat16
    )
    group_loop(lambda g: take_back(gv, gi_ref, g_send, g_recv, g))
    all_loop(lambda p: grad_copy(me, p).wait_recv())
    own_grad.wait()
    for c in range(chan_count):
        for q in range(peers):
            total = gf_ref[c * seq_count + q]
            for which in range(1, LAYERS):
                total = total + gf_ref[c * seq_count + which * peers + q]
            kept_part = total[:, :share]
            for d in range(1, chan_count):
                kept_part = jnp.where(chan == d, total[:, d * share : (d + 1) * share], kept_part)
            at = (c * peers + q) * groups
            grad_ref[at : at + groups, :] = kept_part

    def drain(g):
        peer_loop(lambda p: forward(x_ref, xs, x_send, x_recv, g, p, spot).wait_send())
        peer_loop(lambda p: forward(u_loc, us, u_send, u_recv, g, p, spot).wait_send())
        peer_loop(lambda p: backward(cv, conv_in, c_send, c_recv, g, p, spot).wait_send())
        peer_loop(lambda p: backward(gv, gi_ref, g_send, g_recv, g, p, spot).wait_send())

        @pl.when(layer == 0)
        def _():
            hop(xs, g, 0, 1).wait_send()

        @pl.when(layer == 1)
        def _():
            hop(xs, g, 0, 1).wait_send()
            hop(xs, g, 1, 1).wait_send()
            hand(g, -1).wait_send()

        @pl.when(layer == 2)
        def _():
            hop(us, g, 2, -1).wait_send()
            hop(us, g, 3, -1).wait_send()
            hand(g, 1).wait_send()

        @pl.when(layer == 3)
        def _():
            hop(us, g, 3, -1).wait_send()

    group_loop(drain)
    all_loop(lambda p: filt_copy(p, me).wait_send())
    all_loop(lambda p: grad_copy(p, me).wait_send())


def layered_shards(inputs, gating, grad_out, filters):
    seq_count = lax.axis_size("seq")
    chan_count = lax.axis_size("chan")
    chan_rows, block = inputs.shape
    everyone = seq_count * chan_count
    peers = seq_count // LAYERS
    groups = chan_rows // peers // GROUP_WIDTH
    length = block * seq_count
    rows = length // TILE * GROUP_WIDTH
    layer_rows = rows // LAYERS
    vmem = pl.BlockSpec(memory_space=pltpu.VMEM)
    hbm = pl.BlockSpec(memory_space=pltpu.HBM)
    pair = pltpu.SemaphoreType.DMA((groups, peers))
    stacked = pltpu.SemaphoreType.DMA((groups, LAYERS))
    single = pltpu.SemaphoreType.DMA((groups,))
    many = pltpu.SemaphoreType.DMA((everyone,))
    return pl.pallas_call(
        functools.partial(layered_kernel, seq_count, chan_count),
        out_shape=(
            jax.ShapeDtypeStruct((chan_rows, block), jnp.bfloat16),
            jax.ShapeDtypeStruct((chan_rows, block), jnp.bfloat16),
            jax.ShapeDtypeStruct(filters.shape, jnp.float32),
        ),
        in_specs=[hbm, hbm, hbm, vmem],
        out_specs=(vmem, vmem, vmem),
        scratch_shapes=[
            pltpu.VMEM((chan_rows, block), jnp.bfloat16),
            pltpu.VMEM((chan_rows, block), jnp.bfloat16),
            pltpu.VMEM((chan_count * peers, groups, block), jnp.float32),
            pltpu.VMEM((everyone, groups, block), jnp.float32),
            pltpu.VMEM((chan_rows, block), jnp.bfloat16),
            pltpu.VMEM((groups, rows, TILE), jnp.bfloat16),
            pltpu.VMEM((groups, 2 * rows, TILE), jnp.bfloat16),
            pltpu.VMEM((everyone, groups, block), jnp.float32),
            pltpu.VMEM((groups, layer_rows, TILE), jnp.bfloat16),
            pltpu.VMEM((groups, layer_rows, TILE), jnp.bfloat16),
            pltpu.VMEM((rows, TILE), jnp.float32),
            pltpu.VMEM((rows, TILE), jnp.float32),
            pltpu.VMEM((chan_rows, block), jnp.bfloat16),
            pltpu.VMEM((seq_count, groups, block), jnp.float32),
            pltpu.VMEM((groups, layer_rows, TILE), jnp.float32),
            pltpu.VMEM((groups, layer_rows, TILE), jnp.float32),
            pltpu.VMEM((groups, layer_rows, TILE), jnp.float32),
        ]
        + [pair] * 8
        + [stacked] * 2
        + [single] * 2
        + [many] * 4
        + [pltpu.SemaphoreType.DMA((2,))],
        compiler_params=pltpu.CompilerParams(
            collective_id=0, has_side_effects=True, vmem_limit_bytes=40 * 1024 * 1024
        ),
    )(inputs, gating, grad_out, filters)


def solution(mesh):
    placed = (P("chan", "seq"), P("chan", "seq"), P("chan", "seq"), P(None, ("seq", "chan")))
    layered = mesh.shape["seq"] == 16 and mesh.shape["chan"] == 2
    return jax.shard_map(
        layered_shards if layered else shards,
        mesh=mesh,
        in_specs=placed,
        out_specs=(P("chan", "seq"), P("chan", "seq"), P(None, ("seq", "chan"))),
        check_vma=False,
    )
```
